32 devices in a mesh: section: 4 (over y, x), dp: 4 (over z), mp: 2 (over core).
Axes of the slice: x: 2, y: 2, z: 4, core: 2. Of those that a mesh axis runs over, the one named last changes fastest.
Arguments:
- encoded: float32 [8, 64, 4096], P('dp', None, ('section', 'mp')), may hold values from -6 to 6
- counts: int32 [8], replicated, may hold values from 1 to 64, 384 in all
- owner: int32 [8], replicated, may hold values from 0 to 3, as said below
- w_key: bfloat16 [4, 4096, 2048], P('section', 'dp', 'mp'), may hold values from -0.09375 to 0.09375
- w_value: bfloat16 [4, 4096, 2048], P('section', 'dp', 'mp'), may hold values from -0.09375 to 0.09375
- queries: bfloat16 [4, 16, 128, 2048], P('section', 'dp', None, 'mp'), may hold values from -6 to 6
- grad_out: bfloat16 [4, 16, 128, 2048], P('section', 'dp', None, 'mp'), may hold values from -6 to 6
- dec_mask: int32 [16, 128], P('dp'), may hold values 0 or 1
Outputs:
- attn_out: bfloat16 [4, 16, 128, 2048], P('section', 'dp', None, 'mp')
- d_encoded: float32 [8, 64, 4096], P('dp', None, ('section', 'mp'))
The draws below stay inside these ranges and needn't reach their ends.
Inputs may be any that keep to these rules, and one draw needn't show every extreme that they name: Each owner holds at most 4 dialogues and some owner holds exactly 4.
All inputs are finite; a program needn't handle non-finite values. No bound on the sum of `dec_mask` on one device may be relied on, other than what follows from the above.
Results may differ from the reference program's by a relative error of at most 0.014.
Values may be sent and summed in bfloat16 or wider, within the bound.
A program may use at most 128 MiB of HBM per device.

```python
import math
import jax
import jax.numpy as jnp
import numpy as np
from jax import lax

D = 4096
HEADS = 8
HEAD_DIM = 256
DLG_DEV = 2
CAP = 4
ENC_LEN = 64
DEC_LEN = 128
DIALOGS = 8
SLOTS = 16
N_SECTION = 4
N_DP = 4


def draw_owner(key, part):
    first_key, second_key, third_key = jax.random.split(jax.random.fold_in(key, 11), 3)
    dialog_count = N_DP * DLG_DEV
    hot_owner = jax.random.randint(first_key, (), 0, N_DP).astype(jnp.int32)
    sources = jax.random.permutation(second_key, N_DP).astype(jnp.int32)
    dialog_ids = jnp.arange(dialog_count, dtype=jnp.int32)
    is_hot = (dialog_ids // DLG_DEV == sources[0]) | (dialog_ids == sources[1] * DLG_DEV) | (dialog_ids == sources[2] * DLG_DEV)
    hot_rank = jnp.cumsum(is_hot.astype(jnp.int32)) - 1
    shuffled = jax.random.permutation(third_key, dialog_count).astype(jnp.int32)
    sort_keys = jnp.where(is_hot, hot_rank - dialog_count, shuffled)
    ordering = jnp.argsort(sort_keys, stable=True).astype(jnp.int32)
    offset_rest = dialog_ids - CAP
    pos_owner = jnp.where(dialog_ids < CAP, hot_owner, (hot_owner + 1 + offset_rest % (N_DP - 1)) % N_DP).astype(jnp.int32)
    return jnp.zeros((dialog_count,), jnp.int32).at[ordering].set(pos_owner)


def with_ends(result, rng, least, largest):
    extent = result.shape
    place = [jax.random.randint(jax.random.fold_in(rng, axis), (), 0, extent[axis]) for axis in range(len(extent))]
    result = result.at[tuple(place)].set(least)
    longest = extent.index(max(extent))
    place[longest] = (place[longest] + 1) % extent[longest]
    return result.at[tuple(place)].set(largest)


def shard_levels(key, dims, cuts, low, top_value):
    def one(dim, blocks):
        steps = jax.random.uniform(jax.random.fold_in(jax.random.fold_in(key, 6), dim), (blocks,), jnp.float32, low / len(cuts), top_value / len(cuts))
        return jnp.repeat(jnp.exp(steps), dims[dim] // blocks).reshape((-1,) + (1,) * (len(dims) - dim - 1))

    loudness = one(*cuts[0])
    for cut in cuts[1:]:
        loudness = loudness * one(*cut)
    return loudness


def profile(amount, total, most, lean):
    weights = [(1 << 20) // math.isqrt(standing ** lean) + 1 for standing in range(2, amount + 1)]
    spare, holding = total - most - (amount - 1), [1] * (amount - 1)
    while spare > 0:
        movable = [i for i in range(amount - 1) if holding[i] < most]
        mass, remaining = sum([weights[i] for i in movable]), spare
        for i in movable:
            more = min(most - holding[i], max(1, remaining * weights[i] // mass), spare)
            holding[i] = holding[i] + more
            spare = spare - more
    return np.array([most] + holding)


def ragged(stream_key, number_of, total, limit, lean):
    if number_of == 2:
        one = jax.random.randint(stream_key, (), max(1, total - limit), min(limit, total - 1) + 1)
        return jnp.stack([one, total - one])
    sizes = jnp.asarray(profile(number_of, total, limit, lean), jnp.int32)
    pairs = (number_of - 1) // 2
    giver, receiver = sizes[1:1 + 2 * pairs:2], sizes[2:2 + 2 * pairs:2]
    room = jnp.minimum(giver - 1, limit - receiver)
    passed = jax.random.randint(jax.random.fold_in(stream_key, 1), (pairs,), 0, 1 << 20) % (room + 1)
    sizes = sizes.at[1:1 + 2 * pairs:2].set(giver - passed).at[2:2 + 2 * pairs:2].set(receiver + passed)
    return sizes[jax.random.permutation(jax.random.fold_in(stream_key, 2), number_of)]


def bell_draw(stream_key, shape, width, bound, cuts=(), kind=jnp.bfloat16):
    level = shard_levels(stream_key, shape, cuts, -0.22, 0.18) if cuts else 1.0
    result = jax.random.normal(stream_key, shape, jnp.float32) * width * level
    return jnp.minimum(jnp.maximum(result, -bound), bound).astype(kind)


def setup_inputs(seed: int = 0) -> dict:
    seeds = jax.random.split(jax.random.key(seed), 9)
    return {
        "encoded": bell_draw(seeds[0], (DIALOGS, ENC_LEN, D), 1.0, 6.0, ((0, 4), (2, 8)), jnp.float32),
        "counts": ragged(seeds[1], DIALOGS, DIALOGS * ENC_LEN * 3 // 4, ENC_LEN, 2).astype(jnp.int32),
        "owner": draw_owner(jax.random.fold_in(seeds[8], 71), 0),
        "w_key": bell_draw(seeds[3], (N_SECTION, D, HEADS * HEAD_DIM), D ** -0.5, 0.09375, ((0, 4), (1, 4), (2, 2))),
        "w_value": bell_draw(seeds[4], (N_SECTION, D, HEADS * HEAD_DIM), D ** -0.5, 0.09375, ((0, 4), (1, 4), (2, 2))),
        "queries": bell_draw(seeds[5], (N_SECTION, SLOTS, DEC_LEN, HEADS * HEAD_DIM), 1.0, 6.0, ((0, 4), (1, 4), (3, 2))),
        "grad_out": bell_draw(seeds[6], (N_SECTION, SLOTS, DEC_LEN, HEADS * HEAD_DIM), 1.0, 6.0, ((0, 4), (1, 4), (3, 2))),
        "dec_mask": with_ends((jax.random.randint(seeds[7], (SLOTS, DEC_LEN), 0, 4) < 3).astype(jnp.int32), jax.random.fold_in(seeds[7], 1), 0, 1),
    }


def attend(query_rows, key_rows, value_rows, grad_rows, slot_length, slot_live, answer_mask):
    slot_count, query_len, head_width = query_rows.shape
    key_len = key_rows.shape[1]
    head_count = head_width // HEAD_DIM
    score_scale = HEAD_DIM ** -0.5
    query_heads = query_rows.reshape(slot_count, query_len, head_count, HEAD_DIM).astype(jnp.float32)
    key_heads = key_rows.reshape(slot_count, key_len, head_count, HEAD_DIM).astype(jnp.float32)
    value_heads = value_rows.reshape(slot_count, key_len, head_count, HEAD_DIM).astype(jnp.float32)
    masked_grad = grad_rows * answer_mask.astype(jnp.bfloat16)[:, :, None]
    grad_heads = masked_grad.reshape(slot_count, query_len, head_count, HEAD_DIM).astype(jnp.float32)
    scores = jnp.einsum("cqhd,ckhd->chqk", query_heads, key_heads) * score_scale
    inside = jnp.arange(key_len, dtype=jnp.int32)[None, None, None, :] < slot_length[:, None, None, None]
    unnormed = jnp.where(inside, jnp.exp(scores), 0.0)
    attention = unnormed / (jnp.sum(unnormed, axis=-1, keepdims=True) + (1.0 - slot_live)[:, None, None, None])
    attn_probs = attention.astype(jnp.bfloat16)
    attended = jnp.einsum("chqk,ckhd->cqhd", attn_probs.astype(jnp.float32), value_heads).astype(jnp.bfloat16)
    grad_values = jnp.einsum("chqk,cqhd->ckhd", attn_probs.astype(jnp.float32), grad_heads).astype(jnp.bfloat16)
    grad_probs = jnp.einsum("cqhd,ckhd->chqk", grad_heads, value_heads)
    grad_scores = (attention * (grad_probs - jnp.sum(attention * grad_probs, axis=-1, keepdims=True))).astype(jnp.bfloat16)
    grad_keys = (jnp.einsum("chqk,cqhd->ckhd", grad_scores.astype(jnp.float32), query_heads) * score_scale).astype(jnp.bfloat16)
    return (attended.reshape(slot_count, query_len, head_width),
            grad_keys.reshape(slot_count, key_len, head_width),
            grad_values.reshape(slot_count, key_len, head_width))


def reference(encoded, counts, owner, w_key, w_value, queries, grad_out, dec_mask):
    dialog_ids = jnp.arange(DIALOGS, dtype=jnp.int32)
    is_mine = (owner[None, :] == jnp.arange(N_DP, dtype=jnp.int32)[:, None]).astype(jnp.int32)
    position = jnp.cumsum(is_mine, axis=1) - 1
    picked = is_mine[:, None, :] * (position[:, None, :] == jnp.arange(CAP, dtype=jnp.int32)[None, :, None]).astype(jnp.int32)
    slot_dialog = jnp.sum(picked * dialog_ids[None, None, :], axis=2).reshape(SLOTS).astype(jnp.int32)
    slot_valid = jnp.sum(picked, axis=2).reshape(SLOTS).astype(jnp.int32)
    slot_length = jnp.take(counts, slot_dialog) * slot_valid
    slot_live = slot_valid.astype(jnp.float32)
    slot_keep = slot_valid.astype(jnp.bfloat16)[:, None, None]
    encoded_bf = encoded.astype(jnp.bfloat16).reshape(DIALOGS * ENC_LEN, D)
    head_width = HEADS * HEAD_DIM

    def one_layer(accumulated, pieces):
        key_w, value_w, query_rows, grad_rows = pieces
        key_rows = jnp.dot(encoded_bf, key_w, preferred_element_type=jnp.float32).astype(jnp.bfloat16).reshape(DIALOGS, ENC_LEN, head_width)
        value_rows = jnp.dot(encoded_bf, value_w, preferred_element_type=jnp.float32).astype(jnp.bfloat16).reshape(DIALOGS, ENC_LEN, head_width)
        slot_keys = jnp.take(key_rows, slot_dialog, axis=0) * slot_keep
        slot_values = jnp.take(value_rows, slot_dialog, axis=0) * slot_keep
        attended, grad_keys, grad_values = attend(query_rows, slot_keys, slot_values, grad_rows, slot_length, slot_live, dec_mask)
        dialog_keys = jnp.zeros((DIALOGS, ENC_LEN, head_width), jnp.bfloat16).at[slot_dialog].add(grad_keys * slot_keep)
        dialog_values = jnp.zeros((DIALOGS, ENC_LEN, head_width), jnp.bfloat16).at[slot_dialog].add(grad_values * slot_keep)
        layer_term = jnp.dot(dialog_keys.reshape(-1, head_width), key_w.T, preferred_element_type=jnp.float32)
        layer_term = layer_term + jnp.dot(dialog_values.reshape(-1, head_width), value_w.T, preferred_element_type=jnp.float32)
        return accumulated + layer_term, attended

    start = jnp.zeros((DIALOGS * ENC_LEN, D), jnp.float32)
    accumulated, attn_out = lax.scan(one_layer, start, (w_key, w_value, queries, grad_out))
    return attn_out, accumulated.reshape(DIALOGS, ENC_LEN, D)
```

```python
import functools

import jax
import jax.numpy as jnp
from jax import lax
from jax.experimental import pallas as pl
from jax.experimental.pallas import tpu as pltpu
from jax.sharding import PartitionSpec as P

HEAD_DIM = 256
MESH = pl.DeviceIdType.MESH
SUB = 2
F32 = jnp.float32
BF16 = jnp.bfloat16


def dot(left, right, left_dim, right_dim):
    return lax.dot_general(
        left, right, (((left_dim,), (right_dim,)), ((), ())), preferred_element_type=F32
    )


def kernel(
    dims,
    counts,
    owner,
    encoded,
    w_key,
    w_value,
    queries,
    grad_out,
    mask,
    attn_out,
    d_encoded,
    table,
    weights,
    enc_cast,
    enc_all,
    part,
    fwd_recv,
    fwd_send,
    own_grad,
    bwd_recv,
    bwd_send,
    acc,
    d_send,
    d_recv,
    d_fin,
    d_arrived,
    w_sem,
    swap_send,
    swap_recv,
    self_sem,
    enc_send_sem,
    enc_recv_sem,
    fwd_send_sem,
    fwd_recv_sem,
    bwd_send_sem,
    bwd_recv_sem,
    d_send_sem,
    d_recv_sem,
):
    sections, groups, cores = dims
    section = lax.axis_index("section")
    p = lax.axis_index("dp")
    core = lax.axis_index("mp")
    fold = sections // groups
    plane = sections * cores
    me = section * cores + core
    local_count, key_len, feat = encoded.shape
    dialogs = local_count * groups
    block_rows = local_count * key_len
    cap = queries.shape[0]
    heads = queries.shape[2] // HEAD_DIM
    per = dialogs // SUB
    pieces = 2 * heads * SUB
    scale = HEAD_DIM ** (-0.5)

    to_section, to_p = p * fold + lax.rem(section, fold), section // fold
    from_section, from_p = p * fold + lax.rem(section, fold), section // fold
    stays = section // fold == p

    def region(index):
        s, m = index // cores, lax.rem(index, cores)
        rows = pl.multiple_of((s // fold) * block_rows, block_rows)
        cols = pl.multiple_of((lax.rem(s, fold) * cores + m) * feat, feat)
        return pl.ds(rows, block_rows), pl.ds(cols, feat)

    copies = []
    for h in range(heads):
        for kv, ref in enumerate((w_key, w_value)):
            copy = pltpu.make_async_copy(
                ref.at[:, pl.ds(h * HEAD_DIM, HEAD_DIM)],
                weights.at[2 * h + kv],
                w_sem.at[2 * h + kv],
            )
            copy.start()
            copies.append(copy)

    barrier = pltpu.get_barrier_semaphore()

    def greet(s, z, m):
        pl.semaphore_signal(barrier, inc=1, device_id=(s, z, m), device_id_type=MESH)

    @pl.when(jnp.logical_not(stays))
    def _():
        greet(to_section, to_p, core)

    @pl.when(p > 0)
    def _():
        greet(section, p - 1, core)

    @pl.when(p < groups - 1)
    def _():
        greet(section, p + 1, core)

    @pl.loop(1, plane)
    def _(i):
        peer = lax.rem(me + i, plane)
        greet(peer // cores, p, lax.rem(peer, cores))

    for a in range(local_count):
        enc_cast[pl.ds(a * key_len, key_len), :] = encoded[a].astype(BF16)

    taken = jnp.int32(0)
    slot_dialog = [jnp.int32(0)] * cap
    slot_valid = [jnp.int32(0)] * cap
    slot_length = [jnp.int32(0)] * cap
    for d in range(dialogs):
        mine = (owner[d] == p).astype(jnp.int32)
        table[3 * cap + d] = jnp.where(mine == 1, jnp.minimum(taken, cap), cap)
        for c in range(cap):
            hit = mine * (taken == c).astype(jnp.int32)
            slot_dialog[c] = slot_dialog[c] + hit * d
            slot_valid[c] = slot_valid[c] + hit
            slot_length[c] = slot_length[c] + hit * counts[d]
        taken = taken + mine
    for c in range(cap):
        table[c] = slot_dialog[c]
        table[cap + c] = slot_valid[c]
        table[2 * cap + c] = slot_length[c]

    acc[...] = jnp.zeros_like(acc)
    own_grad[:, cap] = jnp.zeros((own_grad.shape[0],) + own_grad.shape[2:], BF16)

    pl.semaphore_wait(
        barrier,
        plane
        - 1
        + jnp.where(stays, 0, 1)
        + jnp.where(p > 0, 1, 0)
        + jnp.where(p < groups - 1, 1, 0),
    )

    target = to_section * cores + core
    t_rows, t_cols = region(target)
    m_rows, m_cols = region(me)

    def swap_copy():
        return pltpu.make_async_remote_copy(
            src_ref=enc_cast,
            dst_ref=enc_all.at[t_rows, t_cols],
            send_sem=swap_send.at[0],
            recv_sem=swap_recv.at[0],
            device_id=(to_section, to_p, core),
            device_id_type=MESH,
        )

    @pl.when(stays)
    def _():
        copy = pltpu.make_async_copy(enc_cast, enc_all.at[m_rows, m_cols], self_sem.at[0])
        copy.start()
        copy.wait()

    @pl.when(jnp.logical_not(stays))
    def _():
        swap_copy().start()
        pltpu.make_async_remote_copy(
            src_ref=enc_cast,
            dst_ref=enc_all.at[m_rows, m_cols],
            send_sem=swap_send.at[0],
            recv_sem=swap_recv.at[0],
            device_id=(from_section, from_p, core),
            device_id_type=MESH,
        ).wait_recv()

    def plane_copy(peer):
        return pltpu.make_async_remote_copy(
            src_ref=enc_all.at[m_rows, m_cols],
            dst_ref=enc_all.at[m_rows, m_cols],
            send_sem=enc_send_sem.at[peer],
            recv_sem=enc_recv_sem.at[me],
            device_id=(peer // cores, p, lax.rem(peer, cores)),
            device_id_type=MESH,
        )

    def plane_arrival(peer):
        rows, cols = region(peer)
        return pltpu.make_async_remote_copy(
            src_ref=enc_all.at[rows, cols],
            dst_ref=enc_all.at[rows, cols],
            send_sem=enc_send_sem.at[peer],
            recv_sem=enc_recv_sem.at[peer],
            device_id=(peer // cores, p, lax.rem(peer, cores)),
            device_id_type=MESH,
        )

    @pl.loop(1, plane)
    def _(i):
        plane_copy(lax.rem(me + i, plane)).start()

    for copy in copies:
        copy.wait()

    @pl.loop(1, plane)
    def _(i):
        plane_arrival(lax.rem(me + plane - i, plane)).wait_recv()

    def hop(recv, send, send_sem, recv_sem, way, j):
        other = p + 1 if way == 0 else p - 1
        return pltpu.make_async_remote_copy(
            src_ref=send.at[way, j],
            dst_ref=recv.at[way, j],
            send_sem=send_sem.at[way, j],
            recv_sem=recv_sem.at[way, j],
            device_id=(section, other, core),
            device_id_type=MESH,
        )

    def is_first(way):
        return p == 0 if way == 0 else p == groups - 1

    def is_last(way):
        return p == groups - 1 if way == 0 else p == 0

    fwd_hop = functools.partial(hop, fwd_recv, fwd_send, fwd_send_sem, fwd_recv_sem)
    bwd_hop = functools.partial(hop, bwd_recv, bwd_send, bwd_send_sem, bwd_recv_sem)

    def own_rows(j):
        sub = lax.rem(j, SUB)
        return [own_grad[j // SUB, table[3 * cap + sub * per + i]] for i in range(per)]

    def far(way):
        return p if way == 0 else groups - 1 - p

    def inside(j):
        return jnp.logical_and(j >= 0, j < pieces)

    def project(j):
        rows = pl.multiple_of(lax.rem(j, SUB) * (per * key_len), per * key_len)
        product = dot(enc_all[pl.ds(rows, per * key_len), :], weights[j // SUB], 1, 0)
        part[j] = product.astype(BF16).reshape(per, key_len, HEAD_DIM)

    def attend(h):
        cols = pl.ds(pl.multiple_of(h * HEAD_DIM, HEAD_DIM), HEAD_DIM)
        for c in range(cap):
            d = table[c]
            live = table[cap + c]
            length = table[2 * cap + c]
            keep = live.astype(F32)
            keys = (part[2 * h * SUB + d // per, lax.rem(d, per)].astype(F32) * keep).astype(BF16)
            values = (
                part[(2 * h + 1) * SUB + d // per, lax.rem(d, per)].astype(F32) * keep
            ).astype(BF16)
            q = queries[c, :, cols]
            g = (grad_out[c, :, cols].astype(F32) * mask[c]).astype(BF16)
            scores = dot(q, keys, 1, 1) * scale
            ok = lax.broadcasted_iota(jnp.int32, scores.shape, 1) < length
            unnormed = jnp.where(ok, jnp.exp(scores), 0.0)
            attention = unnormed / (jnp.sum(unnormed, axis=1, keepdims=True) + (1.0 - keep))
            probs = attention.astype(BF16)
            attn_out[c, :, cols] = dot(probs, values, 1, 0).astype(BF16)
            own_grad[2 * h + 1, c] = dot(probs, g, 0, 0).astype(BF16)
            grad_probs = dot(g, values, 1, 1)
            grad_scores = (
                attention
                * (grad_probs - jnp.sum(attention * grad_probs, axis=1, keepdims=True))
            ).astype(BF16)
            own_grad[2 * h, c] = (dot(grad_scores, q, 0, 0) * scale).astype(BF16)

    ready = 2 * SUB - 1 + groups - 1
    steps = pieces + ready + groups

    @pl.loop(0, steps)
    def _(t):
        @pl.when(t < pieces)
        def _():
            project(t)

        for way in range(2):
            j = t - far(way)

            @pl.when(inside(j))
            def _(way=way, j=j):
                @pl.when(is_first(way))
                def _():
                    fwd_send[way, j] = part[j]

                @pl.when(jnp.logical_not(is_first(way)))
                def _():
                    fwd_hop(way, j).wait_recv()

                @pl.when(jnp.logical_not(jnp.logical_or(is_first(way), is_last(way))))
                def _():
                    fwd_send[way, j] = (
                        part[j].astype(F32) + fwd_recv[way, j].astype(F32)
                    ).astype(BF16)

                @pl.when(jnp.logical_not(is_last(way)))
                def _():
                    fwd_hop(way, j).start()

        whole = t - (groups - 1)

        @pl.when(inside(whole))
        def _():
            @pl.when(p == 0)
            def _():
                part[whole] = (
                    part[whole].astype(F32) + fwd_recv[1, whole].astype(F32)
                ).astype(BF16)

            @pl.when(p == groups - 1)
            def _():
                part[whole] = (
                    part[whole].astype(F32) + fwd_recv[0, whole].astype(F32)
                ).astype(BF16)

            @pl.when(jnp.logical_and(p > 0, p < groups - 1))
            def _():
                part[whole] = (
                    part[whole].astype(F32)
                    + fwd_recv[0, whole].astype(F32)
                    + fwd_recv[1, whole].astype(F32)
                ).astype(BF16)

            @pl.when(lax.rem(whole, 2 * SUB) == 2 * SUB - 1)
            def _():
                attend(whole // (2 * SUB))

        for way in range(2):
            j = t - ready - far(way)

            @pl.when(inside(j))
            def _(way=way, j=j):
                @pl.when(is_first(way))
                def _():
                    for i, rows in enumerate(own_rows(j)):
                        bwd_send[way, j, i] = rows

                @pl.when(jnp.logical_not(is_first(way)))
                def _():
                    bwd_hop(way, j).wait_recv()

                @pl.when(jnp.logical_not(jnp.logical_or(is_first(way), is_last(way))))
                def _():
                    for i, rows in enumerate(own_rows(j)):
                        bwd_send[way, j, i] = rows + bwd_recv[way, j, i]

                @pl.when(jnp.logical_not(is_last(way)))
                def _():
                    bwd_hop(way, j).start()

        done = t - ready - (groups - 1)

        @pl.when(inside(done))
        def _():
            base = pl.multiple_of(lax.rem(done, SUB) * (per * key_len), per * key_len)

            @pl.when(p == 0)
            def _():
                for i, rows in enumerate(own_rows(done)):
                    part[done, i] = rows + bwd_recv[1, done, i]

            @pl.when(p == groups - 1)
            def _():
                for i, rows in enumerate(own_rows(done)):
                    part[done, i] = rows + bwd_recv[0, done, i]

            @pl.when(jnp.logical_and(p > 0, p < groups - 1))
            def _():
                for i, rows in enumerate(own_rows(done)):
                    part[done, i] = rows + bwd_recv[0, done, i] + bwd_recv[1, done, i]

            grads = part[done].reshape(per * key_len, HEAD_DIM)
            acc[pl.ds(base, per * key_len), :] += dot(grads, weights[done // SUB], 1, 1)

    @pl.loop(0, pieces)
    def _(j):
        for way in range(2):

            @pl.when(jnp.logical_not(is_last(way)))
            def _(way=way):
                fwd_hop(way, j).wait_send()
                bwd_hop(way, j).wait_send()

    d_send[...] = acc[...].astype(BF16)

    def term_copy(peer):
        rows, cols = region(peer)
        return pltpu.make_async_remote_copy(
            src_ref=d_send.at[rows, cols],
            dst_ref=d_recv.at[me],
            send_sem=d_send_sem.at[peer],
            recv_sem=d_recv_sem.at[me],
            device_id=(peer // cores, p, lax.rem(peer, cores)),
            device_id_type=MESH,
        )

    def term_arrival(peer):
        rows, cols = region(peer)
        return pltpu.make_async_remote_copy(
            src_ref=d_send.at[rows, cols],
            dst_ref=d_recv.at[peer],
            send_sem=d_send_sem.at[peer],
            recv_sem=d_recv_sem.at[peer],
            device_id=(peer // cores, p, lax.rem(peer, cores)),
            device_id_type=MESH,
        )

    @pl.loop(1, plane)
    def _(i):
        term_copy(lax.rem(me + i, plane)).start()

    total = acc.at[m_rows, m_cols]

    @pl.loop(1, plane)
    def _(i):
        peer = lax.rem(me + plane - i, plane)
        term_arrival(peer).wait_recv()
        total[...] += d_recv[peer].astype(F32)

    d_fin[...] = total[...].astype(BF16)

    def back_copy():
        return pltpu.make_async_remote_copy(
            src_ref=d_fin,
            dst_ref=d_arrived,
            send_sem=swap_send.at[1],
            recv_sem=swap_recv.at[1],
            device_id=(from_section, from_p, core),
            device_id_type=MESH,
        )

    @pl.when(stays)
    def _():
        for a in range(local_count):
            d_encoded[a] = d_fin[pl.ds(a * key_len, key_len), :].astype(F32)

    @pl.when(jnp.logical_not(stays))
    def _():
        back_copy().start()
        back_copy().wait_recv()
        for a in range(local_count):
            d_encoded[a] = d_arrived[pl.ds(a * key_len, key_len), :].astype(F32)

    @pl.loop(1, plane)
    def _(i):
        peer = lax.rem(me + i, plane)
        plane_copy(peer).wait_send()
        term_copy(peer).wait_send()

    @pl.when(jnp.logical_not(stays))
    def _():
        swap_copy().wait_send()
        back_copy().wait_send()


def body(dims, encoded, counts, owner, w_key, w_value, queries, grad_out, dec_mask):
    sections, groups, cores = dims
    local_count, key_len, feat = encoded.shape
    dialogs = local_count * groups
    cap, query_len, width = queries.shape[1:]
    model_rows = w_key.shape[1]
    heads = width // HEAD_DIM
    per = dialogs // SUB
    pieces = 2 * heads * SUB
    plane = sections * cores
    block_rows = local_count * key_len
    stream = pltpu.VMEM((2, pieces, per, key_len, HEAD_DIM), BF16)
    dma = pltpu.SemaphoreType.DMA
    vmem = pl.BlockSpec(memory_space=pltpu.VMEM)
    smem = pl.BlockSpec(memory_space=pltpu.SMEM)
    hbm = pl.BlockSpec(memory_space=pl.ANY)
    mask = dec_mask.astype(F32)[:, :, None]
    attended, d_encoded = pl.pallas_call(
        functools.partial(kernel, dims),
        out_shape=(
            jax.ShapeDtypeStruct((cap, query_len, width), BF16),
            jax.ShapeDtypeStruct((local_count, key_len, feat), F32),
        ),
        in_specs=[smem, smem, vmem, hbm, hbm, vmem, vmem, vmem],
        out_specs=(vmem, vmem),
        scratch_shapes=[
            pltpu.SMEM((3 * cap + dialogs,), jnp.int32),
            pltpu.VMEM((2 * heads, model_rows, HEAD_DIM), BF16),
            pltpu.VMEM((block_rows, feat), BF16),
            pltpu.VMEM((dialogs * key_len, model_rows), BF16),
            pltpu.VMEM((pieces, per, key_len, HEAD_DIM), BF16),
            stream,
            stream,
            pltpu.VMEM((2 * heads, cap + 1, key_len, HEAD_DIM), BF16),
            stream,
            stream,
            pltpu.VMEM((dialogs * key_len, model_rows), F32),
            pltpu.VMEM((dialogs * key_len, model_rows), BF16),
            pltpu.VMEM((plane, block_rows, feat), BF16),
            pltpu.VMEM((block_rows, feat), BF16),
            pltpu.VMEM((block_rows, feat), BF16),
            dma((2 * heads,)),
            dma((2,)),
            dma((2,)),
            dma((1,)),
            dma((plane,)),
            dma((plane,)),
            dma((2, pieces)),
            dma((2, pieces)),
            dma((2, pieces)),
            dma((2, pieces)),
            dma((plane,)),
            dma((plane,)),
        ],
        compiler_params=pltpu.CompilerParams(
            collective_id=0, has_side_effects=True, vmem_limit_bytes=60 * 1024 * 1024
        ),
    )(counts, owner, encoded, w_key[0], w_value[0], queries[0], grad_out[0], mask)
    return (attended[None], d_encoded)


def solution(mesh):
    placed = (
        P("dp", None, ("section", "mp")),
        P(),
        P(),
        P("section", "dp", "mp"),
        P("section", "dp", "mp"),
        P("section", "dp", None, "mp"),
        P("section", "dp", None, "mp"),
        P("dp", None),
    )
    dims = tuple(mesh.shape[name] for name in ("section", "dp", "mp"))
    return jax.shard_map(
        functools.partial(body, dims),
        mesh=mesh,
        in_specs=placed,
        out_specs=(P("section", "dp", None, "mp"), P("dp", None, ("section", "mp"))),
        check_vma=False,
    )
```

```python
import functools

import jax
import jax.numpy as jnp
from jax import lax
from jax.experimental import pallas as pl
from jax.experimental.pallas import tpu as pltpu
from jax.sharding import PartitionSpec as P

HEAD_DIM = 256
MESH = pl.DeviceIdType.MESH
F32 = jnp.float32
BF16 = jnp.bfloat16


def dot(left, right, left_dim, right_dim):
    return lax.dot_general(
        left, right, (((left_dim,), (right_dim,)), ((), ())), preferred_element_type=F32
    )


def kernel(
    dims,
    counts,
    owner,
    encoded,
    w_key,
    w_value,
    queries,
    grad_out,
    mask,
    attn_out,
    d_encoded,
    table,
    weights,
    enc_cast,
    enc_all,
    part,
    recv,
    send,
    own_grad,
    acc,
    d_send,
    d_pair,
    d_mid,
    d_recv,
    d_fin,
    d_arrived,
    w_sem,
    swap_send,
    swap_recv,
    self_sem,
    enc_send_sem,
    enc_pass_sem,
    enc_recv_sem,
    send_sem,
    recv_sem,
    pair_send_sem,
    pair_recv_sem,
    d_send_sem,
    d_recv_sem,
):
    sections, groups, cores = dims
    section = lax.axis_index("section")
    p = lax.axis_index("dp")
    core = lax.axis_index("mp")
    fold = sections // groups
    local_count, key_len, feat = encoded.shape
    dialogs = local_count * groups
    block_rows = local_count * key_len
    cap = queries.shape[0]
    heads = queries.shape[2] // HEAD_DIM
    per = local_count
    subs = groups
    pieces = heads * subs
    lag = 2 * subs
    others = cores - 1
    scale = HEAD_DIM ** (-0.5)

    swap_section, swap_p = p * fold + lax.rem(section, fold), section // fold
    stays = section // fold == p

    def region(s, m):
        rows = pl.multiple_of((s // fold) * block_rows, block_rows)
        cols = pl.multiple_of((lax.rem(s, fold) * cores + m) * feat, feat)
        return pl.ds(rows, block_rows), pl.ds(cols, feat)

    def remote(src, dst, out_sem, in_sem, device):
        return pltpu.make_async_remote_copy(
            src_ref=src,
            dst_ref=dst,
            send_sem=out_sem,
            recv_sem=in_sem,
            device_id=device,
            device_id_type=MESH,
        )

    barrier = pltpu.get_barrier_semaphore()

    def greet(s, z, m):
        pl.semaphore_signal(barrier, inc=1, device_id=(s, z, m), device_id_type=MESH)

    @pl.when(jnp.logical_not(stays))
    def _():
        greet(swap_section, swap_p, core)

    @pl.when(p > 0)
    def _():
        greet(section, p - 1, core)

    @pl.when(p < groups - 1)
    def _():
        greet(section, p + 1, core)

    @pl.loop(1, sections)
    def _(i):
        greet(lax.rem(section + i, sections), p, core)

    for j in range(1, cores):
        greet(section, p, lax.rem(core + j, cores))

    copies = []
    for h in range(heads):
        for kv, ref in enumerate((w_key, w_value)):
            copy = pltpu.make_async_copy(
                ref.at[:, pl.ds(h * HEAD_DIM, HEAD_DIM)],
                weights.at[2 * h + kv],
                w_sem.at[2 * h + kv],
            )
            copy.start()
            copies.append(copy)

    for a in range(local_count):
        enc_cast[pl.ds(a * key_len, key_len), :] = encoded[a].astype(BF16)

    pl.semaphore_wait(
        barrier,
        sections
        - 1
        + others
        + jnp.where(stays, 0, 1)
        + jnp.where(p > 0, 1, 0)
        + jnp.where(p < groups - 1, 1, 0),
    )

    m_rows, m_cols = region(section, core)
    mine_there = region(swap_section, core)

    def swap_copy():
        return remote(
            enc_cast,
            enc_all.at[mine_there[0], mine_there[1]],
            swap_send.at[0],
            swap_recv.at[0],
            (swap_section, swap_p, core),
        )

    @pl.when(stays)
    def _():
        copy = pltpu.make_async_copy(enc_cast, enc_all.at[m_rows, m_cols], self_sem.at[0])
        copy.start()
        copy.wait()

    @pl.when(jnp.logical_not(stays))
    def _():
        swap_copy().start()

    taken = jnp.int32(0)
    slot_dialog = [jnp.int32(0)] * cap
    slot_valid = [jnp.int32(0)] * cap
    slot_length = [jnp.int32(0)] * cap
    for d in range(dialogs):
        mine = (owner[d] == p).astype(jnp.int32)
        table[3 * cap + d] = jnp.where(mine == 1, jnp.minimum(taken, cap), cap)
        for c in range(cap):
            hit = mine * (taken == c).astype(jnp.int32)
            slot_dialog[c] = slot_dialog[c] + hit * d
            slot_valid[c] = slot_valid[c] + hit
            slot_length[c] = slot_length[c] + hit * counts[d]
        taken = taken + mine
    for c in range(cap):
        table[c] = slot_dialog[c]
        table[cap + c] = slot_valid[c]
        table[2 * cap + c] = slot_length[c]

    acc[...] = jnp.zeros_like(acc)
    own_grad[...] = jnp.zeros_like(own_grad)

    @pl.when(jnp.logical_not(stays))
    def _():
        remote(
            enc_cast,
            enc_all.at[m_rows, m_cols],
            swap_send.at[0],
            swap_recv.at[0],
            (swap_section, swap_p, core),
        ).wait_recv()

    def block_copy(s, out_sem, device):
        rows, cols = region(s[0], s[1])
        return remote(
            enc_all.at[rows, cols],
            enc_all.at[rows, cols],
            out_sem,
            enc_recv_sem.at[s[0] * cores + s[1]],
            device,
        )

    def spread(i):
        peer = lax.rem(section + i, sections)
        return block_copy((section, core), enc_send_sem.at[peer], (peer, p, core))

    def pass_on(s, j):
        return block_copy(
            (s, core),
            enc_pass_sem.at[s * others + j - 1],
            (section, p, lax.rem(core + j, cores)),
        )

    @pl.loop(1, sections)
    def _(i):
        spread(i).start()

    for j in range(1, cores):
        pass_on(section, j).start()

    for copy in copies:
        copy.wait()

    @pl.loop(1, sections)
    def _(i):
        s = lax.rem(section + sections - i, sections)
        block_copy((s, core), enc_send_sem.at[s], (s, p, core)).wait_recv()
        for j in range(1, cores):
            pass_on(s, j).start()

    @pl.loop(0, sections)
    def _(i):
        s = lax.rem(section + sections - i, sections)
        for j in range(1, cores):
            m = lax.rem(core + j, cores)
            block_copy((s, m), enc_send_sem.at[s], (section, p, m)).wait_recv()

    def hop(way, r):
        return remote(
            send.at[way, r],
            recv.at[way, r],
            send_sem.at[way, r],
            recv_sem.at[way, r],
            (section, p + 1 if way == 0 else p - 1, core),
        )

    def is_first(way):
        return p == 0 if way == 0 else p == groups - 1

    def is_last(way):
        return p == groups - 1 if way == 0 else p == 0

    def far(way):
        return p if way == 0 else groups - 1 - p

    def within(r, count):
        return jnp.logical_and(r >= 0, r < count)

    def ahead(way, r, i):
        d = lax.rem(r, subs) * per + i
        delta = owner[d] - p if way == 0 else p - owner[d]
        return jnp.full((key_len, HEAD_DIM), delta, jnp.int32)

    def own_rows(b, kv, i):
        return own_grad[b // subs, kv, table[3 * cap + lax.rem(b, subs) * per + i]].astype(F32)

    def project(h):
        for kv in range(2):
            product = dot(enc_all[...], weights[2 * h + kv], 1, 0).astype(BF16)
            part[pl.ds(h * subs, subs), kv] = product.reshape(subs, per, key_len, HEAD_DIM)

    def attend(h):
        cols = pl.ds(pl.multiple_of(h * HEAD_DIM, HEAD_DIM), HEAD_DIM)
        for c in range(cap):
            d = table[c]
            keep = table[cap + c].astype(F32)
            length = table[2 * cap + c]
            keys = (part[h * subs + d // per, 0, lax.rem(d, per)].astype(F32) * keep).astype(BF16)
            values = (
                part[h * subs + d // per, 1, lax.rem(d, per)].astype(F32) * keep
            ).astype(BF16)
            q = queries[c, :, cols]
            g = (grad_out[c, :, cols].astype(F32) * mask[c]).astype(BF16)
            scores = dot(q, keys, 1, 1) * scale
            ok = lax.broadcasted_iota(jnp.int32, scores.shape, 1) < length
            unnormed = jnp.where(ok, jnp.exp(scores), 0.0)
            attention = unnormed / (jnp.sum(unnormed, axis=1, keepdims=True) + (1.0 - keep))
            probs = attention.astype(BF16)
            attn_out[c, :, cols] = dot(probs, values, 1, 0).astype(BF16)
            own_grad[h, 1, c] = dot(probs, g, 0, 0).astype(BF16)
            grad_probs = dot(g, values, 1, 1)
            grad_scores = (
                attention
                * (grad_probs - jnp.sum(attention * grad_probs, axis=1, keepdims=True))
            ).astype(BF16)
            own_grad[h, 0, c] = (dot(grad_scores, q, 0, 0) * scale).astype(BF16)

    rounds = pieces + lag
    steps = rounds + groups - 1

    @pl.loop(0, steps)
    def _(t):
        @pl.when(jnp.logical_and(t < pieces, lax.rem(t, subs) == 0))
        def _():
            project(t // subs)

        for way in range(2):
            r = t - far(way)

            @pl.when(within(r, rounds))
            def _(way=way, r=r):
                fwd, bwd = jnp.minimum(r, pieces - 1), jnp.maximum(r - lag, 0)

                @pl.when(is_first(way))
                def _():
                    for kv in range(2):
                        for i in range(per):
                            send[way, r, kv, i] = jnp.where(
                                ahead(way, r, i) > 0,
                                part[fwd, kv, i].astype(F32),
                                own_rows(bwd, kv, i),
                            ).astype(BF16)

                @pl.when(jnp.logical_not(is_first(way)))
                def _():
                    hop(way, r).wait_recv()

                @pl.when(jnp.logical_not(jnp.logical_or(is_first(way), is_last(way))))
                def _():
                    for kv in range(2):
                        for i in range(per):
                            where_to = ahead(way, r, i)
                            came = recv[way, r, kv, i].astype(F32)
                            send[way, r, kv, i] = jnp.where(
                                where_to > 0,
                                came + part[fwd, kv, i].astype(F32),
                                jnp.where(where_to == 0, own_rows(bwd, kv, i), came),
                            ).astype(BF16)

                @pl.when(jnp.logical_not(is_last(way)))
                def _():
                    hop(way, r).start()

        whole = t - (groups - 1)

        @pl.when(within(whole, pieces))
        def _():
            @pl.when(p == 0)
            def _():
                part[whole] = (part[whole].astype(F32) + recv[1, whole].astype(F32)).astype(BF16)

            @pl.when(p == groups - 1)
            def _():
                part[whole] = (part[whole].astype(F32) + recv[0, whole].astype(F32)).astype(BF16)

            @pl.when(jnp.logical_and(p > 0, p < groups - 1))
            def _():
                part[whole] = (
                    part[whole].astype(F32)
                    + recv[0, whole].astype(F32)
                    + recv[1, whole].astype(F32)
                ).astype(BF16)

            @pl.when(lax.rem(whole, subs) == subs - 1)
            def _():
                attend(whole // subs)

        done = t - (groups - 1) - lag

        @pl.when(within(done, pieces))
        def _():
            r = done + lag

            def collect(below, above):
                for kv in range(2):
                    for i in range(per):
                        where_to = ahead(0, r, i)
                        rows = own_rows(done, kv, i)
                        if below:
                            rows = jnp.where(where_to < 0, recv[0, r, kv, i].astype(F32), rows)
                        if above:
                            rows = jnp.where(where_to > 0, recv[1, r, kv, i].astype(F32), rows)
                        part[done, kv, i] = rows.astype(BF16)

            @pl.when(p == 0)
            def _():
                collect(False, True)

            @pl.when(p == groups - 1)
            def _():
                collect(True, False)

            @pl.when(jnp.logical_and(p > 0, p < groups - 1))
            def _():
                collect(True, True)

            @pl.when(lax.rem(done, subs) == subs - 1)
            def _():
                h = done // subs
                for kv in range(2):
                    grads = part[pl.ds(h * subs, subs), kv].reshape(dialogs * key_len, HEAD_DIM)
                    acc[...] += dot(grads, weights[2 * h + kv], 1, 1)

    d_send[...] = acc[...].astype(BF16)

    def pair_copy(s, j):
        m = lax.rem(core + j, cores)
        rows, cols = region(s, m)
        k = s * others + j - 1
        return remote(
            d_send.at[rows, cols], d_pair.at[k], pair_send_sem.at[k], pair_recv_sem.at[k],
            (section, p, m),
        )

    def term_copy(s):
        return remote(
            d_mid.at[s], d_recv.at[section], d_send_sem.at[s], d_recv_sem.at[section],
            (s, p, core),
        )

    @pl.loop(1, sections + 1)
    def _(i):
        for j in range(1, cores):
            pair_copy(lax.rem(section + i, sections), j).start()

    def paired(s):
        rows, cols = region(s, core)
        total = acc[rows, cols]
        for j in range(1, cores):
            pair_copy(s, j).wait_recv()
            total = total + d_pair[s * others + j - 1].astype(F32)
        return total

    @pl.loop(1, sections)
    def _(i):
        s = lax.rem(section + i, sections)
        d_mid[s] = paired(s).astype(BF16)
        term_copy(s).start()

    acc[m_rows, m_cols] = paired(section)

    @pl.loop(1, sections)
    def _(i):
        s = lax.rem(section + sections - i, sections)
        remote(
            d_mid.at[s], d_recv.at[s], d_send_sem.at[s], d_recv_sem.at[s], (s, p, core)
        ).wait_recv()
        acc[m_rows, m_cols] += d_recv[s].astype(F32)

    d_fin[...] = acc[m_rows, m_cols].astype(BF16)

    def back_copy():
        return remote(
            d_fin, d_arrived, swap_send.at[1], swap_recv.at[1], (swap_section, swap_p, core)
        )

    @pl.when(stays)
    def _():
        for a in range(local_count):
            d_encoded[a] = d_fin[pl.ds(a * key_len, key_len), :].astype(F32)

    @pl.when(jnp.logical_not(stays))
    def _():
        back_copy().start()

    @pl.loop(0, rounds)
    def _(r):
        for way in range(2):

            @pl.when(jnp.logical_not(is_last(way)))
            def _(way=way):
                hop(way, r).wait_send()

    @pl.loop(1, sections)
    def _(i):
        spread(i).wait_send()
        term_copy(lax.rem(section + i, sections)).wait_send()

    @pl.loop(0, sections)
    def _(s):
        for j in range(1, cores):
            pass_on(s, j).wait_send()
            pair_copy(s, j).wait_send()

    @pl.when(jnp.logical_not(stays))
    def _():
        swap_copy().wait_send()
        back_copy().wait()
        for a in range(local_count):
            d_encoded[a] = d_arrived[pl.ds(a * key_len, key_len), :].astype(F32)


def body(dims, encoded, counts, owner, w_key, w_value, queries, grad_out, dec_mask):
    sections, groups, cores = dims
    local_count, key_len, feat = encoded.shape
    dialogs = local_count * groups
    cap, query_len, width = queries.shape[1:]
    model_rows = w_key.shape[1]
    heads = width // HEAD_DIM
    per = local_count
    pieces = heads * groups
    rounds = pieces + 2 * groups
    others = cores - 1
    block_rows = local_count * key_len
    item = (2, per, key_len, HEAD_DIM)
    dma = pltpu.SemaphoreType.DMA
    vmem = pl.BlockSpec(memory_space=pltpu.VMEM)
    smem = pl.BlockSpec(memory_space=pltpu.SMEM)
    hbm = pl.BlockSpec(memory_space=pl.ANY)
    mask = dec_mask.astype(F32)[:, :, None]
    attended, d_encoded = pl.pallas_call(
        functools.partial(kernel, dims),
        out_shape=(
            jax.ShapeDtypeStruct((cap, query_len, width), BF16),
            jax.ShapeDtypeStruct((local_count, key_len, feat), F32),
        ),
        in_specs=[smem, smem, vmem, hbm, hbm, vmem, vmem, vmem],
        out_specs=(vmem, vmem),
        scratch_shapes=[
            pltpu.SMEM((3 * cap + dialogs,), jnp.int32),
            pltpu.VMEM((2 * heads, model_rows, HEAD_DIM), BF16),
            pltpu.VMEM((block_rows, feat), BF16),
            pltpu.VMEM((dialogs * key_len, model_rows), BF16),
            pltpu.VMEM((pieces,) + item, BF16),
            pltpu.VMEM((2, rounds) + item, BF16),
            pltpu.VMEM((2, rounds) + item, BF16),
            pltpu.VMEM((heads, 2, cap + 1, key_len, HEAD_DIM), BF16),
            pltpu.VMEM((dialogs * key_len, model_rows), F32),
            pltpu.VMEM((dialogs * key_len, model_rows), BF16),
            pltpu.VMEM((sections * others, block_rows, feat), BF16),
            pltpu.VMEM((sections, block_rows, feat), BF16),
            pltpu.VMEM((sections, block_rows, feat), BF16),
            pltpu.VMEM((block_rows, feat), BF16),
            pltpu.VMEM((block_rows, feat), BF16),
            dma((2 * heads,)),
            dma((2,)),
            dma((2,)),
            dma((1,)),
            dma((sections,)),
            dma((sections * others,)),
            dma((sections * cores,)),
            dma((2, rounds)),
            dma((2, rounds)),
            dma((sections * others,)),
            dma((sections * others,)),
            dma((sections,)),
            dma((sections,)),
        ],
        compiler_params=pltpu.CompilerParams(
            collective_id=0, has_side_effects=True, vmem_limit_bytes=60 * 1024 * 1024
        ),
    )(counts, owner, encoded, w_key[0], w_value[0], queries[0], grad_out[0], mask)
    return (attended[None], d_encoded)


def solution(mesh):
    placed = (
        P("dp", None, ("section", "mp")),
        P(),
        P(),
        P("section", "dp", "mp"),
        P("section", "dp", "mp"),
        P("section", "dp", None, "mp"),
        P("section", "dp", None, "mp"),
        P("dp", None),
    )
    dims = tuple(mesh.shape[name] for name in ("section", "dp", "mp"))
    return jax.shard_map(
        functools.partial(body, dims),
        mesh=mesh,
        in_specs=placed,
        out_specs=(P("section", "dp", None, "mp"), P("dp", None, ("section", "mp"))),
        check_vma=False,
    )
```

```python
import functools

import jax
import jax.numpy as jnp
from jax import lax
from jax.experimental import pallas as pl
from jax.experimental.pallas import tpu as pltpu
from jax.sharding import PartitionSpec as P

HEAD_DIM = 256
MESH = pl.DeviceIdType.MESH
F32 = jnp.float32
BF16 = jnp.bfloat16


def skew(hops):
    return (5 * hops + 1) // 3


def lag_of(groups):
    return pl.cdiv(groups - 1 + skew(groups - 1), groups) * groups


def dot(left, right, left_dim, right_dim):
    return lax.dot_general(
        left, right, (((left_dim,), (right_dim,)), ((), ())), preferred_element_type=F32
    )


def kernel(
    dims,
    counts,
    owner,
    encoded,
    w_key,
    w_value,
    queries,
    grad_out,
    mask,
    attn_out,
    d_encoded,
    table,
    weights,
    enc_cast,
    enc_all,
    part,
    recv,
    send,
    own_grad,
    acc,
    d_send,
    d_pair,
    d_mid,
    d_recv,
    d_fin,
    d_arrived,
    w_sem,
    swap_send,
    swap_recv,
    self_sem,
    enc_send_sem,
    enc_pass_sem,
    enc_recv_sem,
    send_sem,
    recv_sem,
    pair_send_sem,
    pair_recv_sem,
    d_send_sem,
    d_recv_sem,
):
    sections, groups, cores = dims
    section = lax.axis_index("section")
    p = lax.axis_index("dp")
    core = lax.axis_index("mp")
    fold = sections // groups
    local_count, key_len, feat = encoded.shape
    dialogs = local_count * groups
    block_rows = local_count * key_len
    cap = queries.shape[0]
    heads = queries.shape[2] // HEAD_DIM
    per = local_count
    subs = groups
    pieces = heads * subs
    lag = lag_of(groups)
    late = skew(groups - 1)
    others = cores - 1
    scale = HEAD_DIM ** (-0.5)

    swap_section, swap_p = p * fold + lax.rem(section, fold), section // fold
    stays = section // fold == p

    def region(s, m):
        rows = pl.multiple_of((s // fold) * block_rows, block_rows)
        cols = pl.multiple_of((lax.rem(s, fold) * cores + m) * feat, feat)
        return pl.ds(rows, block_rows), pl.ds(cols, feat)

    def remote(src, dst, out_sem, in_sem, device):
        return pltpu.make_async_remote_copy(
            src_ref=src,
            dst_ref=dst,
            send_sem=out_sem,
            recv_sem=in_sem,
            device_id=device,
            device_id_type=MESH,
        )

    barrier = pltpu.get_barrier_semaphore()

    def greet(s, z, m):
        pl.semaphore_signal(barrier, inc=1, device_id=(s, z, m), device_id_type=MESH)

    @pl.when(jnp.logical_not(stays))
    def _():
        greet(swap_section, swap_p, core)

    @pl.when(p > 0)
    def _():
        greet(section, p - 1, core)

    @pl.when(p < groups - 1)
    def _():
        greet(section, p + 1, core)

    @pl.loop(1, sections)
    def _(i):
        greet(lax.rem(section + i, sections), p, core)

    for j in range(1, cores):
        greet(section, p, lax.rem(core + j, cores))

    copies = []
    for h in range(heads):
        for kv, ref in enumerate((w_key, w_value)):
            copy = pltpu.make_async_copy(
                ref.at[:, pl.ds(h * HEAD_DIM, HEAD_DIM)],
                weights.at[2 * h + kv],
                w_sem.at[2 * h + kv],
            )
            copy.start()
            copies.append(copy)

    for a in range(local_count):
        enc_cast[pl.ds(a * key_len, key_len), :] = encoded[a].astype(BF16)

    pl.semaphore_wait(
        barrier,
        sections
        - 1
        + others
        + jnp.where(stays, 0, 1)
        + jnp.where(p > 0, 1, 0)
        + jnp.where(p < groups - 1, 1, 0),
    )

    m_rows, m_cols = region(section, core)
    mine_there = region(swap_section, core)

    def swap_copy():
        return remote(
            enc_cast,
            enc_all.at[mine_there[0], mine_there[1]],
            swap_send.at[0],
            swap_recv.at[0],
            (swap_section, swap_p, core),
        )

    @pl.when(stays)
    def _():
        copy = pltpu.make_async_copy(enc_cast, enc_all.at[m_rows, m_cols], self_sem.at[0])
        copy.start()
        copy.wait()

    @pl.when(jnp.logical_not(stays))
    def _():
        swap_copy().start()

    taken = jnp.int32(0)
    slot_dialog = [jnp.int32(0)] * cap
    slot_valid = [jnp.int32(0)] * cap
    slot_length = [jnp.int32(0)] * cap
    for d in range(dialogs):
        mine = (owner[d] == p).astype(jnp.int32)
        table[3 * cap + d] = jnp.where(mine == 1, jnp.minimum(taken, cap), cap)
        for c in range(cap):
            hit = mine * (taken == c).astype(jnp.int32)
            slot_dialog[c] = slot_dialog[c] + hit * d
            slot_valid[c] = slot_valid[c] + hit
            slot_length[c] = slot_length[c] + hit * counts[d]
        taken = taken + mine
    for c in range(cap):
        table[c] = slot_dialog[c]
        table[cap + c] = slot_valid[c]
        table[2 * cap + c] = slot_length[c]

    acc[...] = jnp.zeros_like(acc)
    own_grad[...] = jnp.zeros_like(own_grad)

    @pl.when(jnp.logical_not(stays))
    def _():
        remote(
            enc_cast,
            enc_all.at[m_rows, m_cols],
            swap_send.at[0],
            swap_recv.at[0],
            (swap_section, swap_p, core),
        ).wait_recv()

    def block_copy(s, out_sem, device):
        rows, cols = region(s[0], s[1])
        return remote(
            enc_all.at[rows, cols],
            enc_all.at[rows, cols],
            out_sem,
            enc_recv_sem.at[s[0] * cores + s[1]],
            device,
        )

    def spread(i):
        peer = lax.rem(section + i, sections)
        return block_copy((section, core), enc_send_sem.at[peer], (peer, p, core))

    def pass_on(s, j):
        return block_copy(
            (s, core),
            enc_pass_sem.at[s * others + j - 1],
            (section, p, lax.rem(core + j, cores)),
        )

    @pl.loop(1, sections)
    def _(i):
        spread(i).start()

    for j in range(1, cores):
        pass_on(section, j).start()

    for copy in copies:
        copy.wait()

    @pl.loop(1, sections)
    def _(i):
        s = lax.rem(section + sections - i, sections)
        block_copy((s, core), enc_send_sem.at[s], (s, p, core)).wait_recv()
        for j in range(1, cores):
            pass_on(s, j).start()

    @pl.loop(0, sections)
    def _(i):
        s = lax.rem(section + sections - i, sections)
        for j in range(1, cores):
            m = lax.rem(core + j, cores)
            block_copy((s, m), enc_send_sem.at[s], (section, p, m)).wait_recv()

    def hop(way, r):
        return remote(
            send.at[way, r],
            recv.at[way, r],
            send_sem.at[way, r],
            recv_sem.at[way, r],
            (section, p + 1 if way == 0 else p - 1, core),
        )

    def is_first(way):
        return p == 0 if way == 0 else p == groups - 1

    def is_last(way):
        return p == groups - 1 if way == 0 else p == 0

    def far(way):
        return skew(p if way == 0 else groups - 1 - p)

    def within(r, count):
        return jnp.logical_and(r >= 0, r < count)

    def ahead(way, r, i):
        d = lax.rem(r, subs) * per + i
        delta = owner[d] - p if way == 0 else p - owner[d]
        return jnp.full((key_len, HEAD_DIM), delta, jnp.int32)

    def own_rows(b, kv, i):
        return own_grad[b // subs, kv, table[3 * cap + lax.rem(b, subs) * per + i]].astype(F32)

    def project(h):
        for kv in range(2):
            product = dot(enc_all[...], weights[2 * h + kv], 1, 0).astype(BF16)
            part[pl.ds(h * subs, subs), kv] = product.reshape(subs, per, key_len, HEAD_DIM)

    def attend(h):
        cols = pl.ds(pl.multiple_of(h * HEAD_DIM, HEAD_DIM), HEAD_DIM)
        for c in range(cap):
            d = table[c]
            keep = table[cap + c].astype(F32)
            length = table[2 * cap + c]
            keys = (part[h * subs + d // per, 0, lax.rem(d, per)].astype(F32) * keep).astype(BF16)
            values = (
                part[h * subs + d // per, 1, lax.rem(d, per)].astype(F32) * keep
            ).astype(BF16)
            q = queries[c, :, cols]
            g = (grad_out[c, :, cols].astype(F32) * mask[c]).astype(BF16)
            scores = dot(q, keys, 1, 1) * scale
            ok = lax.broadcasted_iota(jnp.int32, scores.shape, 1) < length
            unnormed = jnp.where(ok, jnp.exp(scores), 0.0)
            attention = unnormed / (jnp.sum(unnormed, axis=1, keepdims=True) + (1.0 - keep))
            probs = attention.astype(BF16)
            attn_out[c, :, cols] = dot(probs, values, 1, 0).astype(BF16)
            own_grad[h, 1, c] = dot(probs, g, 0, 0).astype(BF16)
            grad_probs = dot(g, values, 1, 1)
            grad_scores = (
                attention
                * (grad_probs - jnp.sum(attention * grad_probs, axis=1, keepdims=True))
            ).astype(BF16)
            own_grad[h, 0, c] = (dot(grad_scores, q, 0, 0) * scale).astype(BF16)

    rounds = pieces + lag
    steps = rounds + late

    @pl.loop(0, steps)
    def _(t):
        @pl.when(jnp.logical_and(t < pieces, lax.rem(t, subs) == 0))
        def _():
            project(t // subs)

        for way in range(2):
            r = t - far(way)

            @pl.when(within(r, rounds))
            def _(way=way, r=r):
                fwd, bwd = jnp.minimum(r, pieces - 1), jnp.maximum(r - lag, 0)

                @pl.when(jnp.logical_not(is_first(way)))
                def _():
                    hop(way, r).wait_recv()

                @pl.when(jnp.logical_not(jnp.logical_or(is_first(way), is_last(way))))
                def _(fwd=fwd, bwd=bwd):
                    for kv in range(2):
                        for i in range(per):
                            where_to = ahead(way, r, i)
                            came = recv[way, r, kv, i].astype(F32)
                            send[way, r, kv, i] = jnp.where(
                                where_to > 0,
                                came + part[fwd, kv, i].astype(F32),
                                jnp.where(where_to == 0, own_rows(bwd, kv, i), came),
                            ).astype(BF16)

                    hop(way, r).start()

        whole = t - late

        @pl.when(within(whole, pieces))
        def _():
            @pl.when(p == 0)
            def _():
                part[whole] = (part[whole].astype(F32) + recv[1, whole].astype(F32)).astype(BF16)

            @pl.when(p == groups - 1)
            def _():
                part[whole] = (part[whole].astype(F32) + recv[0, whole].astype(F32)).astype(BF16)

            @pl.when(jnp.logical_and(p > 0, p < groups - 1))
            def _():
                part[whole] = (
                    part[whole].astype(F32)
                    + recv[0, whole].astype(F32)
                    + recv[1, whole].astype(F32)
                ).astype(BF16)

            @pl.when(lax.rem(whole, subs) == subs - 1)
            def _():
                attend(whole // subs)

        for way in range(2):

            @pl.when(jnp.logical_and(is_first(way), t < rounds))
            def _(way=way):
                fwd, bwd = jnp.minimum(t, pieces - 1), jnp.maximum(t - lag, 0)
                for kv in range(2):
                    for i in range(per):
                        send[way, t, kv, i] = jnp.where(
                            ahead(way, t, i) > 0,
                            part[fwd, kv, i].astype(F32),
                            own_rows(bwd, kv, i),
                        ).astype(BF16)
                hop(way, t).start()

        done = t - late - lag

        @pl.when(within(done, pieces))
        def _():
            r = done + lag

            def collect(below, above):
                for kv in range(2):
                    for i in range(per):
                        where_to = ahead(0, r, i)
                        rows = own_rows(done, kv, i)
                        if below:
                            rows = jnp.where(where_to < 0, recv[0, r, kv, i].astype(F32), rows)
                        if above:
                            rows = jnp.where(where_to > 0, recv[1, r, kv, i].astype(F32), rows)
                        part[done, kv, i] = rows.astype(BF16)

            @pl.when(p == 0)
            def _():
                collect(False, True)

            @pl.when(p == groups - 1)
            def _():
                collect(True, False)

            @pl.when(jnp.logical_and(p > 0, p < groups - 1))
            def _():
                collect(True, True)

            @pl.when(lax.rem(done, subs) == subs - 1)
            def _():
                h = done // subs
                for kv in range(2):
                    grads = part[pl.ds(h * subs, subs), kv].reshape(dialogs * key_len, HEAD_DIM)
                    acc[...] += dot(grads, weights[2 * h + kv], 1, 1)

    d_send[...] = acc[...].astype(BF16)

    def pair_copy(s, j):
        m = lax.rem(core + j, cores)
        rows, cols = region(s, m)
        k = s * others + j - 1
        return remote(
            d_send.at[rows, cols], d_pair.at[k], pair_send_sem.at[k], pair_recv_sem.at[k],
            (section, p, m),
        )

    def term_copy(s):
        return remote(
            d_mid.at[s], d_recv.at[section], d_send_sem.at[s], d_recv_sem.at[section],
            (s, p, core),
        )

    @pl.loop(1, sections + 1)
    def _(i):
        for j in range(1, cores):
            pair_copy(lax.rem(section + i, sections), j).start()

    def paired(s):
        rows, cols = region(s, core)
        total = acc[rows, cols]
        for j in range(1, cores):
            pair_copy(s, j).wait_recv()
            total = total + d_pair[s * others + j - 1].astype(F32)
        return total

    @pl.loop(1, sections)
    def _(i):
        s = lax.rem(section + i, sections)
        d_mid[s] = paired(s).astype(BF16)
        term_copy(s).start()

    acc[m_rows, m_cols] = paired(section)

    @pl.loop(1, sections)
    def _(i):
        s = lax.rem(section + sections - i, sections)
        remote(
            d_mid.at[s], d_recv.at[s], d_send_sem.at[s], d_recv_sem.at[s], (s, p, core)
        ).wait_recv()
        acc[m_rows, m_cols] += d_recv[s].astype(F32)

    d_fin[...] = acc[m_rows, m_cols].astype(BF16)

    def back_copy():
        return remote(
            d_fin, d_arrived, swap_send.at[1], swap_recv.at[1], (swap_section, swap_p, core)
        )

    @pl.when(stays)
    def _():
        for a in range(local_count):
            d_encoded[a] = d_fin[pl.ds(a * key_len, key_len), :].astype(F32)

    @pl.when(jnp.logical_not(stays))
    def _():
        back_copy().start()

    @pl.loop(0, rounds)
    def _(r):
        for way in range(2):

            @pl.when(jnp.logical_not(is_last(way)))
            def _(way=way):
                hop(way, r).wait_send()

    @pl.loop(1, sections)
    def _(i):
        spread(i).wait_send()
        term_copy(lax.rem(section + i, sections)).wait_send()

    @pl.loop(0, sections)
    def _(s):
        for j in range(1, cores):
            pass_on(s, j).wait_send()
            pair_copy(s, j).wait_send()

    @pl.when(jnp.logical_not(stays))
    def _():
        swap_copy().wait_send()
        back_copy().wait()
        for a in range(local_count):
            d_encoded[a] = d_arrived[pl.ds(a * key_len, key_len), :].astype(F32)


def body(dims, encoded, counts, owner, w_key, w_value, queries, grad_out, dec_mask):
    sections, groups, cores = dims
    local_count, key_len, feat = encoded.shape
    dialogs = local_count * groups
    cap, query_len, width = queries.shape[1:]
    model_rows = w_key.shape[1]
    heads = width // HEAD_DIM
    per = local_count
    pieces = heads * groups
    rounds = pieces + lag_of(groups)
    others = cores - 1
    block_rows = local_count * key_len
    item = (2, per, key_len, HEAD_DIM)
    dma = pltpu.SemaphoreType.DMA
    vmem = pl.BlockSpec(memory_space=pltpu.VMEM)
    smem = pl.BlockSpec(memory_space=pltpu.SMEM)
    hbm = pl.BlockSpec(memory_space=pl.ANY)
    mask = dec_mask.astype(F32)[:, :, None]
    attended, d_encoded = pl.pallas_call(
        functools.partial(kernel, dims),
        out_shape=(
            jax.ShapeDtypeStruct((cap, query_len, width), BF16),
            jax.ShapeDtypeStruct((local_count, key_len, feat), F32),
        ),
        in_specs=[smem, smem, vmem, hbm, hbm, vmem, vmem, vmem],
        out_specs=(vmem, vmem),
        scratch_shapes=[
            pltpu.SMEM((3 * cap + dialogs,), jnp.int32),
            pltpu.VMEM((2 * heads, model_rows, HEAD_DIM), BF16),
            pltpu.VMEM((block_rows, feat), BF16),
            pltpu.VMEM((dialogs * key_len, model_rows), BF16),
            pltpu.VMEM((pieces,) + item, BF16),
            pltpu.VMEM((2, rounds) + item, BF16),
            pltpu.VMEM((2, rounds) + item, BF16),
            pltpu.VMEM((heads, 2, cap + 1, key_len, HEAD_DIM), BF16),
            pltpu.VMEM((dialogs * key_len, model_rows), F32),
            pltpu.VMEM((dialogs * key_len, model_rows), BF16),
            pltpu.VMEM((sections * others, block_rows, feat), BF16),
            pltpu.VMEM((sections, block_rows, feat), BF16),
            pltpu.VMEM((sections, block_rows, feat), BF16),
            pltpu.VMEM((block_rows, feat), BF16),
            pltpu.VMEM((block_rows, feat), BF16),
            dma((2 * heads,)),
            dma((2,)),
            dma((2,)),
            dma((1,)),
            dma((sections,)),
            dma((sections * others,)),
            dma((sections * cores,)),
            dma((2, rounds)),
            dma((2, rounds)),
            dma((sections * others,)),
            dma((sections * others,)),
            dma((sections,)),
            dma((sections,)),
        ],
        compiler_params=pltpu.CompilerParams(
            collective_id=0, has_side_effects=True, vmem_limit_bytes=60 * 1024 * 1024
        ),
    )(counts, owner, encoded, w_key[0], w_value[0], queries[0], grad_out[0], mask)
    return (attended[None], d_encoded)


def solution(mesh):
    placed = (
        P("dp", None, ("section", "mp")),
        P(),
        P(),
        P("section", "dp", "mp"),
        P("section", "dp", "mp"),
        P("section", "dp", None, "mp"),
        P("section", "dp", None, "mp"),
        P("dp", None),
    )
    dims = tuple(mesh.shape[name] for name in ("section", "dp", "mp"))
    return jax.shard_map(
        functools.partial(body, dims),
        mesh=mesh,
        in_specs=placed,
        out_specs=(P("section", "dp", None, "mp"), P("dp", None, ("section", "mp"))),
        check_vma=False,
    )
```

```python
import functools

import jax
import jax.numpy as jnp
from jax import lax
from jax.experimental import pallas as pl
from jax.experimental.pallas import tpu as pltpu
from jax.sharding import PartitionSpec as P

HEAD_DIM = 256
MESH = pl.DeviceIdType.MESH
F32 = jnp.float32
BF16 = jnp.bfloat16


def skew(hops):
    return (5 * hops + 2) // 3


def lag_of(groups):
    return pl.cdiv(groups - 1 + skew(groups - 1), groups) * groups


def dot(left, right, left_dim, right_dim):
    return lax.dot_general(
        left, right, (((left_dim,), (right_dim,)), ((), ())), preferred_element_type=F32
    )


def kernel(
    dims,
    counts,
    owner,
    encoded,
    w_key,
    w_value,
    queries,
    grad_out,
    mask,
    attn_out,
    d_encoded,
    table,
    weights,
    enc_cast,
    enc_all,
    part,
    recv,
    send,
    own_grad,
    acc,
    d_send,
    d_pair,
    d_mid,
    d_recv,
    d_fin,
    d_arrived,
    w_sem,
    swap_send,
    swap_recv,
    self_sem,
    enc_send_sem,
    enc_pass_sem,
    enc_recv_sem,
    send_sem,
    recv_sem,
    pair_send_sem,
    pair_recv_sem,
    d_send_sem,
    d_recv_sem,
):
    sections, groups, cores = dims
    section = lax.axis_index("section")
    p = lax.axis_index("dp")
    core = lax.axis_index("mp")
    fold = sections // groups
    local_count, key_len, feat = encoded.shape
    dialogs = local_count * groups
    block_rows = local_count * key_len
    cap = queries.shape[0]
    heads = queries.shape[2] // HEAD_DIM
    per = local_count
    subs = groups
    pieces = heads * subs
    lag = lag_of(groups)
    late = skew(groups - 1)
    others = cores - 1
    scale = HEAD_DIM ** (-0.5)

    swap_section, swap_p = p * fold + lax.rem(section, fold), section // fold
    stays = section // fold == p

    def region(s, m):
        rows = pl.multiple_of((s // fold) * block_rows, block_rows)
        cols = pl.multiple_of((lax.rem(s, fold) * cores + m) * feat, feat)
        return pl.ds(rows, block_rows), pl.ds(cols, feat)

    def remote(src, dst, out_sem, in_sem, device):
        return pltpu.make_async_remote_copy(
            src_ref=src,
            dst_ref=dst,
            send_sem=out_sem,
            recv_sem=in_sem,
            device_id=device,
            device_id_type=MESH,
        )

    barrier = pltpu.get_barrier_semaphore()

    def greet(s, z, m):
        pl.semaphore_signal(barrier, inc=1, device_id=(s, z, m), device_id_type=MESH)

    @pl.when(jnp.logical_not(stays))
    def _():
        greet(swap_section, swap_p, core)

    @pl.when(p > 0)
    def _():
        greet(section, p - 1, core)

    @pl.when(p < groups - 1)
    def _():
        greet(section, p + 1, core)

    @pl.loop(1, sections)
    def _(i):
        greet(lax.rem(section + i, sections), p, core)

    for j in range(1, cores):
        greet(section, p, lax.rem(core + j, cores))

    copies = []
    for h in range(heads):
        for kv, ref in enumerate((w_key, w_value)):
            copy = pltpu.make_async_copy(
                ref.at[:, pl.ds(h * HEAD_DIM, HEAD_DIM)],
                weights.at[2 * h + kv],
                w_sem.at[2 * h + kv],
            )
            copy.start()
            copies.append(copy)

    for a in range(local_count):
        enc_cast[pl.ds(a * key_len, key_len), :] = encoded[a].astype(BF16)

    pl.semaphore_wait(
        barrier,
        sections
        - 1
        + others
        + jnp.where(stays, 0, 1)
        + jnp.where(p > 0, 1, 0)
        + jnp.where(p < groups - 1, 1, 0),
    )

    m_rows, m_cols = region(section, core)
    mine_there = region(swap_section, core)

    def swap_copy():
        return remote(
            enc_cast,
            enc_all.at[mine_there[0], mine_there[1]],
            swap_send.at[0],
            swap_recv.at[0],
            (swap_section, swap_p, core),
        )

    @pl.when(stays)
    def _():
        copy = pltpu.make_async_copy(enc_cast, enc_all.at[m_rows, m_cols], self_sem.at[0])
        copy.start()
        copy.wait()

    @pl.when(jnp.logical_not(stays))
    def _():
        swap_copy().start()

    taken = jnp.int32(0)
    slot_dialog = [jnp.int32(0)] * cap
    slot_valid = [jnp.int32(0)] * cap
    slot_length = [jnp.int32(0)] * cap
    for d in range(dialogs):
        mine = (owner[d] == p).astype(jnp.int32)
        table[3 * cap + d] = jnp.where(mine == 1, jnp.minimum(taken, cap), cap)
        for c in range(cap):
            hit = mine * (taken == c).astype(jnp.int32)
            slot_dialog[c] = slot_dialog[c] + hit * d
            slot_valid[c] = slot_valid[c] + hit
            slot_length[c] = slot_length[c] + hit * counts[d]
        taken = taken + mine
    for c in range(cap):
        table[c] = slot_dialog[c]
        table[cap + c] = slot_valid[c]
        table[2 * cap + c] = slot_length[c]

    acc[...] = jnp.zeros_like(acc)
    own_grad[...] = jnp.zeros_like(own_grad)

    @pl.when(jnp.logical_not(stays))
    def _():
        remote(
            enc_cast,
            enc_all.at[m_rows, m_cols],
            swap_send.at[0],
            swap_recv.at[0],
            (swap_section, swap_p, core),
        ).wait_recv()

    def block_copy(s, out_sem, device):
        rows, cols = region(s[0], s[1])
        return remote(
            enc_all.at[rows, cols],
            enc_all.at[rows, cols],
            out_sem,
            enc_recv_sem.at[s[0] * cores + s[1]],
            device,
        )

    def spread(i):
        peer = lax.rem(section + i, sections)
        return block_copy((section, core), enc_send_sem.at[peer], (peer, p, core))

    def pass_on(s, j):
        return block_copy(
            (s, core),
            enc_pass_sem.at[s * others + j - 1],
            (section, p, lax.rem(core + j, cores)),
        )

    @pl.loop(1, sections)
    def _(i):
        spread(i).start()

    for j in range(1, cores):
        pass_on(section, j).start()

    for copy in copies:
        copy.wait()

    @pl.loop(1, sections)
    def _(i):
        s = lax.rem(section + sections - i, sections)
        block_copy((s, core), enc_send_sem.at[s], (s, p, core)).wait_recv()
        for j in range(1, cores):
            pass_on(s, j).start()

    @pl.loop(0, sections)
    def _(i):
        s = lax.rem(section + sections - i, sections)
        for j in range(1, cores):
            m = lax.rem(core + j, cores)
            block_copy((s, m), enc_send_sem.at[s], (section, p, m)).wait_recv()

    def hop(way, r):
        return remote(
            send.at[way, r],
            recv.at[way, r],
            send_sem.at[way, r],
            recv_sem.at[way, r],
            (section, p + 1 if way == 0 else p - 1, core),
        )

    def is_first(way):
        return p == 0 if way == 0 else p == groups - 1

    def is_last(way):
        return p == groups - 1 if way == 0 else p == 0

    def far(way):
        return skew(p if way == 0 else groups - 1 - p)

    def within(r, count):
        return jnp.logical_and(r >= 0, r < count)

    def ahead(way, r, i):
        d = lax.rem(r, subs) * per + i
        delta = owner[d] - p if way == 0 else p - owner[d]
        return jnp.full((key_len, HEAD_DIM), delta, jnp.int32)

    def own_rows(b, kv, i):
        return own_grad[b // subs, kv, table[3 * cap + lax.rem(b, subs) * per + i]].astype(F32)

    def project(h):
        for kv in range(2):
            product = dot(enc_all[...], weights[2 * h + kv], 1, 0).astype(BF16)
            part[pl.ds(h * subs, subs), kv] = product.reshape(subs, per, key_len, HEAD_DIM)

    def attend(h):
        cols = pl.ds(pl.multiple_of(h * HEAD_DIM, HEAD_DIM), HEAD_DIM)
        for c in range(cap):
            d = table[c]
            keep = table[cap + c].astype(F32)
            length = table[2 * cap + c]
            keys = (part[h * subs + d // per, 0, lax.rem(d, per)].astype(F32) * keep).astype(BF16)
            values = (
                part[h * subs + d // per, 1, lax.rem(d, per)].astype(F32) * keep
            ).astype(BF16)
            q = queries[c, :, cols]
            g = (grad_out[c, :, cols].astype(F32) * mask[c]).astype(BF16)
            scores = dot(q, keys, 1, 1) * scale
            ok = lax.broadcasted_iota(jnp.int32, scores.shape, 1) < length
            unnormed = jnp.where(ok, jnp.exp(scores), 0.0)
            attention = unnormed / (jnp.sum(unnormed, axis=1, keepdims=True) + (1.0 - keep))
            probs = attention.astype(BF16)
            attn_out[c, :, cols] = dot(probs, values, 1, 0).astype(BF16)
            own_grad[h, 1, c] = dot(probs, g, 0, 0).astype(BF16)
            grad_probs = dot(g, values, 1, 1)
            grad_scores = (
                attention
                * (grad_probs - jnp.sum(attention * grad_probs, axis=1, keepdims=True))
            ).astype(BF16)
            own_grad[h, 0, c] = (dot(grad_scores, q, 0, 0) * scale).astype(BF16)

    rounds = pieces + lag
    steps = rounds + late

    @pl.loop(0, steps)
    def _(t):
        @pl.when(jnp.logical_and(t < pieces, lax.rem(t, subs) == 0))
        def _():
            project(t // subs)

        for way in range(2):
            r = t - far(way)

            @pl.when(within(r, rounds))
            def _(way=way, r=r):
                fwd, bwd = jnp.minimum(r, pieces - 1), jnp.maximum(r - lag, 0)

                @pl.when(jnp.logical_not(is_first(way)))
                def _():
                    hop(way, r).wait_recv()

                @pl.when(jnp.logical_not(jnp.logical_or(is_first(way), is_last(way))))
                def _(fwd=fwd, bwd=bwd):
                    for kv in range(2):
                        for i in range(per):
                            where_to = ahead(way, r, i)
                            came = recv[way, r, kv, i].astype(F32)
                            send[way, r, kv, i] = jnp.where(
                                where_to > 0,
                                came + part[fwd, kv, i].astype(F32),
                                jnp.where(where_to == 0, own_rows(bwd, kv, i), came),
                            ).astype(BF16)

                    hop(way, r).start()

        whole = t - late

        @pl.when(within(whole, pieces))
        def _():
            @pl.when(p == 0)
            def _():
                part[whole] = (part[whole].astype(F32) + recv[1, whole].astype(F32)).astype(BF16)

            @pl.when(p == groups - 1)
            def _():
                part[whole] = (part[whole].astype(F32) + recv[0, whole].astype(F32)).astype(BF16)

            @pl.when(jnp.logical_and(p > 0, p < groups - 1))
            def _():
                part[whole] = (
                    part[whole].astype(F32)
                    + recv[0, whole].astype(F32)
                    + recv[1, whole].astype(F32)
                ).astype(BF16)

            @pl.when(lax.rem(whole, subs) == subs - 1)
            def _():
                attend(whole // subs)

        for way in range(2):

            @pl.when(jnp.logical_and(is_first(way), t < rounds))
            def _(way=way):
                fwd, bwd = jnp.minimum(t, pieces - 1), jnp.maximum(t - lag, 0)
                for kv in range(2):
                    for i in range(per):
                        send[way, t, kv, i] = jnp.where(
                            ahead(way, t, i) > 0,
                            part[fwd, kv, i].astype(F32),
                            own_rows(bwd, kv, i),
                        ).astype(BF16)
                hop(way, t).start()

        done = t - late - lag

        @pl.when(within(done, pieces))
        def _():
            r = done + lag

            def collect(below, above):
                for kv in range(2):
                    for i in range(per):
                        where_to = ahead(0, r, i)
                        rows = own_rows(done, kv, i)
                        if below:
                            rows = jnp.where(where_to < 0, recv[0, r, kv, i].astype(F32), rows)
                        if above:
                            rows = jnp.where(where_to > 0, recv[1, r, kv, i].astype(F32), rows)
                        part[done, kv, i] = rows.astype(BF16)

            @pl.when(p == 0)
            def _():
                collect(False, True)

            @pl.when(p == groups - 1)
            def _():
                collect(True, False)

            @pl.when(jnp.logical_and(p > 0, p < groups - 1))
            def _():
                collect(True, True)

            @pl.when(lax.rem(done, subs) == subs - 1)
            def _():
                h = done // subs
                for kv in range(2):
                    grads = part[pl.ds(h * subs, subs), kv].reshape(dialogs * key_len, HEAD_DIM)
                    acc[...] += dot(grads, weights[2 * h + kv], 1, 1)

    d_send[...] = acc[...].astype(BF16)

    def pair_copy(s, j):
        m = lax.rem(core + j, cores)
        rows, cols = region(s, m)
        k = s * others + j - 1
        return remote(
            d_send.at[rows, cols], d_pair.at[k], pair_send_sem.at[k], pair_recv_sem.at[k],
            (section, p, m),
        )

    def term_copy(s):
        return remote(
            d_mid.at[s], d_recv.at[section], d_send_sem.at[s], d_recv_sem.at[section],
            (s, p, core),
        )

    @pl.loop(1, sections + 1)
    def _(i):
        for j in range(1, cores):
            pair_copy(lax.rem(section + i, sections), j).start()

    def paired(s):
        rows, cols = region(s, core)
        total = acc[rows, cols]
        for j in range(1, cores):
            pair_copy(s, j).wait_recv()
            total = total + d_pair[s * others + j - 1].astype(F32)
        return total

    @pl.loop(1, sections)
    def _(i):
        s = lax.rem(section + i, sections)
        d_mid[s] = paired(s).astype(BF16)
        term_copy(s).start()

    acc[m_rows, m_cols] = paired(section)

    @pl.loop(1, sections)
    def _(i):
        s = lax.rem(section + sections - i, sections)
        remote(
            d_mid.at[s], d_recv.at[s], d_send_sem.at[s], d_recv_sem.at[s], (s, p, core)
        ).wait_recv()
        acc[m_rows, m_cols] += d_recv[s].astype(F32)

    d_fin[...] = acc[m_rows, m_cols].astype(BF16)

    def back_copy():
        return remote(
            d_fin, d_arrived, swap_send.at[1], swap_recv.at[1], (swap_section, swap_p, core)
        )

    @pl.when(stays)
    def _():
        for a in range(local_count):
            d_encoded[a] = d_fin[pl.ds(a * key_len, key_len), :].astype(F32)

    @pl.when(jnp.logical_not(stays))
    def _():
        back_copy().start()

    @pl.loop(0, rounds)
    def _(r):
        for way in range(2):

            @pl.when(jnp.logical_not(is_last(way)))
            def _(way=way):
                hop(way, r).wait_send()

    @pl.loop(1, sections)
    def _(i):
        spread(i).wait_send()
        term_copy(lax.rem(section + i, sections)).wait_send()

    @pl.loop(0, sections)
    def _(s):
        for j in range(1, cores):
            pass_on(s, j).wait_send()
            pair_copy(s, j).wait_send()

    @pl.when(jnp.logical_not(stays))
    def _():
        swap_copy().wait_send()
        back_copy().wait()
        for a in range(local_count):
            d_encoded[a] = d_arrived[pl.ds(a * key_len, key_len), :].astype(F32)


def body(dims, encoded, counts, owner, w_key, w_value, queries, grad_out, dec_mask):
    sections, groups, cores = dims
    local_count, key_len, feat = encoded.shape
    dialogs = local_count * groups
    cap, query_len, width = queries.shape[1:]
    model_rows = w_key.shape[1]
    heads = width // HEAD_DIM
    per = local_count
    pieces = heads * groups
    rounds = pieces + lag_of(groups)
    others = cores - 1
    block_rows = local_count * key_len
    item = (2, per, key_len, HEAD_DIM)
    dma = pltpu.SemaphoreType.DMA
    vmem = pl.BlockSpec(memory_space=pltpu.VMEM)
    smem = pl.BlockSpec(memory_space=pltpu.SMEM)
    hbm = pl.BlockSpec(memory_space=pl.ANY)
    mask = dec_mask.astype(F32)[:, :, None]
    attended, d_encoded = pl.pallas_call(
        functools.partial(kernel, dims),
        out_shape=(
            jax.ShapeDtypeStruct((cap, query_len, width), BF16),
            jax.ShapeDtypeStruct((local_count, key_len, feat), F32),
        ),
        in_specs=[smem, smem, vmem, hbm, hbm, vmem, vmem, vmem],
        out_specs=(vmem, vmem),
        scratch_shapes=[
            pltpu.SMEM((3 * cap + dialogs,), jnp.int32),
            pltpu.VMEM((2 * heads, model_rows, HEAD_DIM), BF16),
            pltpu.VMEM((block_rows, feat), BF16),
            pltpu.VMEM((dialogs * key_len, model_rows), BF16),
            pltpu.VMEM((pieces,) + item, BF16),
            pltpu.VMEM((2, rounds) + item, BF16),
            pltpu.VMEM((2, rounds) + item, BF16),
            pltpu.VMEM((heads, 2, cap + 1, key_len, HEAD_DIM), BF16),
            pltpu.VMEM((dialogs * key_len, model_rows), F32),
            pltpu.VMEM((dialogs * key_len, model_rows), BF16),
            pltpu.VMEM((sections * others, block_rows, feat), BF16),
            pltpu.VMEM((sections, block_rows, feat), BF16),
            pltpu.VMEM((sections, block_rows, feat), BF16),
            pltpu.VMEM((block_rows, feat), BF16),
            pltpu.VMEM((block_rows, feat), BF16),
            dma((2 * heads,)),
            dma((2,)),
            dma((2,)),
            dma((1,)),
            dma((sections,)),
            dma((sections * others,)),
            dma((sections * cores,)),
            dma((2, rounds)),
            dma((2, rounds)),
            dma((sections * others,)),
            dma((sections * others,)),
            dma((sections,)),
            dma((sections,)),
        ],
        compiler_params=pltpu.CompilerParams(
            collective_id=0, has_side_effects=True, vmem_limit_bytes=60 * 1024 * 1024
        ),
    )(counts, owner, encoded, w_key[0], w_value[0], queries[0], grad_out[0], mask)
    return (attended[None], d_encoded)


def solution(mesh):
    placed = (
        P("dp", None, ("section", "mp")),
        P(),
        P(),
        P("section", "dp", "mp"),
        P("section", "dp", "mp"),
        P("section", "dp", None, "mp"),
        P("section", "dp", None, "mp"),
        P("dp", None),
    )
    dims = tuple(mesh.shape[name] for name in ("section", "dp", "mp"))
    return jax.shard_map(
        functools.partial(body, dims),
        mesh=mesh,
        in_specs=placed,
        out_specs=(P("section", "dp", None, "mp"), P("dp", None, ("section", "mp"))),
        check_vma=False,
    )
```
